32 devices in a mesh: layer: 4 (over x, core), grid: 8 (over z, y).
Axes of the slice: x: 2, y: 2, z: 4, core: 2. Of those that a mesh axis runs over, the one named last changes fastest.
Arguments:
- band_blocks: bfloat16 [80, 9, 128, 128], P('grid'), may hold values from -7 to 7, as said below
- retained: int32 [80, 9], P('grid'), may hold values from 0 to 1, as said below
Outputs:
- purified: bfloat16 [80, 9, 128, 128], P('grid', None, 'layer')
The draws below stay inside these ranges and needn't reach their ends.
Inputs may be any that keep to these rules, and one draw needn't show every extreme that they name: `band_blocks`: the matrix is symmetric: block slot w of block row i equals the transpose of block slot 8 - w of block row (i + w - 4) mod 80. retained[i, w] = 1 exactly when retained[(i + w - 4) mod 80, 8 - w] = 1; the middle slot w = 4 is 1 in every block row.
All inputs are finite; a program needn't handle non-finite values.
Results may differ from the reference program's by a relative error of at most 0.005.
Values may be sent and summed in bfloat16 or wider, within the bound.
A program may use at most 64 MiB of HBM per device.

```python
import jax
import jax.numpy as jnp
from jax import lax

BLOCK = 128
REACH = 4
BAND = 9
STEPS = 2
NB = 80


def mirror_tables():
    row_table = (jnp.arange(NB)[:, None] + jnp.arange(BAND)[None, :] - REACH) % NB
    slot_table = (BAND - 1 - jnp.arange(BAND))[None, :]
    return (row_table.astype(jnp.int32), slot_table.astype(jnp.int32))


def draw_band_blocks(key, part):
    first_key = jax.random.fold_in(key, 11)
    second_key = jax.random.fold_in(key, 12)
    shape = (NB, BAND, BLOCK, BLOCK)
    base = jnp.clip(jax.random.normal(first_key, shape, jnp.float32), -3.5, 3.5)
    extra = jnp.clip(jax.random.normal(second_key, shape, jnp.float32), -3.5, 3.5)
    row_table, slot_table = mirror_tables()
    mirror = jnp.swapaxes(base[row_table, slot_table], 2, 3)
    extra_mirror = jnp.swapaxes(extra[row_table, slot_table], 2, 3)
    joined = 1.026 * (base + mirror) + 0.57275649 * (extra + extra_mirror)
    return jnp.clip(joined, -7.0, 7.0).astype(jnp.bfloat16)


def draw_retained(key, part):
    coin_key = jax.random.fold_in(key, 21)
    coins = jax.random.randint(coin_key, (NB, BAND), 0, 2).astype(jnp.int32)
    row_table, slot_table = mirror_tables()
    joined = jnp.maximum(coins, coins[row_table, slot_table])
    middle = (jnp.arange(BAND) == REACH)[None, :]
    return jnp.where(middle, 1, joined).astype(jnp.int32)


def setup_inputs(seed: int = 0) -> dict:
    seeds = jax.random.split(jax.random.key(seed), 3)
    return {
        "band_blocks": draw_band_blocks(jax.random.fold_in(seeds[2], 71), 0),
        "retained": draw_retained(jax.random.fold_in(seeds[2], 71), 0),
    }


def band_product(left_blocks, right_blocks):
    left_wide = left_blocks.astype(jnp.float32)
    right_wide = right_blocks.astype(jnp.float32)
    total = jnp.zeros(left_blocks.shape, jnp.float32)
    for offset in range(BAND):
        moved = jnp.roll(right_wide, REACH - offset, axis=0)
        lowest = max(0, offset - REACH)
        highest = min(BAND, BAND + offset - REACH)
        source = moved[:, lowest - offset + REACH:highest - offset + REACH]
        product_term = jnp.einsum('nab,nwbc->nwac', left_wide[:, offset], source, precision=lax.Precision.HIGHEST)
        total = total.at[:, lowest:highest].add(product_term)
    return total


def reference(band_blocks, retained):
    kept = (retained != 0)[:, :, None, None]
    current = jnp.where(kept, band_blocks, jnp.zeros_like(band_blocks))
    for repeat in range(STEPS):
        square = jnp.where(kept, band_product(current, current), 0.0).astype(jnp.bfloat16)
        cube = jnp.where(kept, band_product(square, current), 0.0)
        current = ((3.0 * current.astype(jnp.float32) - cube / (4.0 * BAND * BLOCK)) * 0.5).astype(jnp.bfloat16)
    return current
```

```python
import functools

import jax
import jax.numpy as jnp
from jax import lax
from jax.experimental import pallas as pl
from jax.experimental.pallas import tpu as pltpu
from jax.sharding import PartitionSpec as P

MESH = pl.DeviceIdType.MESH


def exchange(dims, x_ref, r_ref, h_ref, r3_ref, send, recv, r_send, r_recv, local):
    layers, grids, rows, reach, piece = dims
    depth = 2 * reach
    q = lax.axis_index("layer")
    g = lax.axis_index("grid")
    right = lax.rem(g + 1, grids)
    left = lax.rem(g + grids - 1, grids)
    far = lax.rem(q + layers // 2, layers)
    near = q + 1 - 2 * lax.rem(q, 2)

    barrier = pltpu.get_barrier_semaphore()
    peers = ((q, left), (q, right), (far, g), (near, g))
    for peer in peers:
        pl.semaphore_signal(barrier, inc=1, device_id=peer, device_id_type=MESH)
    pl.semaphore_wait(barrier, len(peers))

    mine = pl.ds(pl.multiple_of(q * piece, piece), piece)
    fars = pl.ds(pl.multiple_of(far * piece, piece), piece)

    def copy(stage, side, j, source, target, peer):
        return pltpu.make_async_remote_copy(
            src_ref=source,
            dst_ref=target,
            send_sem=send.at[stage, side, j],
            recv_sem=recv.at[stage, side, j],
            device_id=peer,
            device_id_type=MESH,
        )

    copies = {}
    for j in range(depth):
        count = min(reach + 1, depth - j)
        for side in range(2):
            first = rows - depth if side == 0 else 0
            there = h_ref.at[side, j, 0:count, mine, :]
            beyond = h_ref.at[side, j, 0:count, fars, :]
            source = x_ref.at[first + j, reach : reach + count, mine, :]
            copies[0, side, j] = copy(
                0, side, j, source, there, (q, right if side == 0 else left)
            )
            copies[1, side, j] = copy(1, side, j, there, there, (far, g))
            copies[2, side, j] = copy(2, side, j, there, there, (near, g))
            copies[3, side, j] = copy(3, side, j, beyond, beyond, (near, g))
            copies[0, side, j].start()
    flags = []
    for side in range(2):
        flags.append(
            pltpu.make_async_remote_copy(
                src_ref=r_ref,
                dst_ref=r3_ref.at[2 * side],
                send_sem=r_send.at[side],
                recv_sem=r_recv.at[side],
                device_id=(q, right if side == 0 else left),
                device_id_type=MESH,
            )
        )
        flags[side].start()
    own = pltpu.make_async_copy(r_ref, r3_ref.at[1], local)
    own.start()
    for j in range(depth + 1):
        for side in range(2):
            if j < depth:
                copies[0, side, j].wait_recv()
                copies[1, side, j].start()
                copies[2, side, j].start()
            if j > 0:
                copies[1, side, j - 1].wait_recv()
                copies[3, side, j - 1].start()
    for j in range(depth):
        for side in range(2):
            copies[2, side, j].wait_recv()
            copies[3, side, j].wait_recv()
            for stage in range(4):
                copies[stage, side, j].wait_send()
    for flag in flags:
        flag.wait()
    own.wait()


def purify(dims, r3, x_ref, h_ref, o_ref, wide, cur, strip, part, part_square):
    rows, reach, block, piece = dims
    band = 2 * reach + 1
    depth = 2 * reach
    tile = 2 * block
    span = reach // 2
    scale = 1.0 / (4.0 * band * block)
    q = lax.axis_index("layer")
    total = rows + 2 * depth
    tiles = rows // 2
    mids = tiles + 2 * span

    def kept(r, w):
        place = r + rows
        return r3[lax.div(place, rows), lax.rem(place, rows), w] if not isinstance(place, int) else r3[
            place // rows, place % rows, w
        ]

    def masked(value, r, w):
        return jnp.where(kept(r, w) != 0, value, jnp.zeros_like(value))

    def put(r, c, value):
        wide[
            (r + depth) * block : (r + depth + 1) * block,
            (c + depth) * block : (c + depth + 1) * block,
        ] = value

    empty = jnp.zeros((block, block), jnp.bfloat16)
    for t in range(total // 2):
        r = 2 * t - depth
        if r + reach + 1 < rows + depth:
            put(r, r + reach + 1, empty)
        if r - reach >= -depth:
            put(r + 1, r - reach, empty)
    for r in range(rows):
        for w in range(band):
            c = r + w - reach
            value = masked(x_ref[r, w], r, w)
            put(r, c, value)
            if c < 0 or c >= rows:
                put(c, r, value.T)
    for side in range(2):
        for j in range(depth):
            r = j - depth if side == 0 else rows + j
            for s in range(min(reach + 1, depth - j)):
                value = masked(h_ref[side, j, s], r, reach + s)
                put(r, r + s, value)
                if s > 0:
                    put(r + s, r, value.T)

    def ranges(d):
        low = max(0, d - span)
        high = min(2 * span, d + span)
        return low, high + 1

    def step(i, carry):
        top = pl.multiple_of((i + span) * tile, tile)
        left = pl.multiple_of(i * tile, tile)
        for d in range(2 * span + 1):
            low, high = ranges(d)
            inner = pl.ds(left + low * tile, (high - low) * tile)
            columns = pl.ds(left + d * tile, tile)
            product = jnp.dot(
                wide[pl.ds(top, tile), inner],
                wide[inner, columns],
                preferred_element_type=jnp.float32,
            )
            for a in range(2):
                for b in range(2):
                    w = 2 * (d - span) + b - a + reach
                    value = product[a * block : (a + 1) * block, b * block : (b + 1) * block]
                    if 0 <= w < band:
                        value = masked(value, 2 * i - reach + a, w)
                    else:
                        value = jnp.zeros_like(value)
                    strip[
                        a * block : (a + 1) * block,
                        d * tile + b * block : d * tile + (b + 1) * block,
                    ] = value.astype(jnp.bfloat16)
        for d in range(2 * span + 1):
            low, high = ranges(d)
            inner = pl.ds(left + low * tile, (high - low) * tile)
            columns = pl.ds(left + d * tile, tile)
            product = jnp.dot(
                strip[:, low * tile : high * tile],
                wide[inner, columns],
                preferred_element_type=jnp.float32,
            )
            value = (
                3.0 * wide[pl.ds(top, tile), columns].astype(jnp.float32) - product * scale
            ) * 0.5
            for a in range(2):
                for b in range(2):
                    w = 2 * (d - span) + b - a + reach
                    piece_value = value[a * block : (a + 1) * block, b * block : (b + 1) * block]
                    if 0 <= w < band:
                        piece_value = masked(piece_value, 2 * i - reach + a, w)
                    else:
                        piece_value = jnp.zeros_like(piece_value)
                    cur[
                        pl.ds(pl.multiple_of(i * tile + a * block, block), block),
                        pl.ds(pl.multiple_of(left + d * tile + b * block, block), block),
                    ] = piece_value.astype(jnp.bfloat16)
        return carry

    lax.fori_loop(0, mids, step, 0)

    part[...] = jnp.zeros_like(part)
    part_square[...] = jnp.zeros_like(part_square)
    for r in range(rows):
        start = pl.multiple_of((r + reach) * block + q * piece, piece)
        part[r * piece : (r + 1) * piece, r * block : (r + band) * block] = cur[
            pl.ds(start, piece), (r + reach) * block : (r + reach + band) * block
        ]

    def columns_of(c, left):
        low, high = max(0, c - span), min(mids, c + span + 1)
        first, last = max(0, c - 2 * span), min(tiles, c + 1)
        product = jnp.dot(
            left[first * 2 * piece : last * 2 * piece, low * tile : high * tile],
            cur[low * tile : high * tile, (c + span) * tile : (c + span + 1) * tile],
            preferred_element_type=jnp.float32,
        )
        for r in range(2 * first, 2 * last):
            for b in range(2):
                w = 2 * c + b - r
                if 0 <= w < band:
                    at = (r - 2 * first) * piece
                    yield r, w, product[at : at + piece, b * block : (b + 1) * block]

    for c in range(mids):
        for r, w, value in columns_of(c, part):
            part_square[
                r * piece : (r + 1) * piece, (r + w) * block : (r + w + 1) * block
            ] = masked(value, r, w).astype(jnp.bfloat16)
    for c in range(mids):
        for r, w, value in columns_of(c, part_square):
            before = part[r * piece : (r + 1) * piece, (r + w) * block : (r + w + 1) * block]
            after = (3.0 * before.astype(jnp.float32) - value * scale) * 0.5
            o_ref[r, w] = masked(after, r, w).astype(jnp.bfloat16)


def per_device(layers, grids, band_blocks, retained):
    rows, band, block, _ = band_blocks.shape
    reach = (band - 1) // 2
    depth = 2 * reach
    piece = block // layers
    dtype = band_blocks.dtype
    anywhere = pl.BlockSpec(memory_space=pl.ANY)
    halo, flags = pl.pallas_call(
        functools.partial(exchange, (layers, grids, rows, reach, piece)),
        out_shape=(
            jax.ShapeDtypeStruct((2, depth, reach + 1, block, block), dtype),
            jax.ShapeDtypeStruct((3, rows, band), retained.dtype),
        ),
        in_specs=[anywhere, anywhere],
        out_specs=(anywhere, anywhere),
        scratch_shapes=[
            pltpu.SemaphoreType.DMA((4, 2, depth)),
            pltpu.SemaphoreType.DMA((4, 2, depth)),
            pltpu.SemaphoreType.DMA((2,)),
            pltpu.SemaphoreType.DMA((2,)),
            pltpu.SemaphoreType.DMA,
        ],
        compiler_params=pltpu.CompilerParams(collective_id=0, has_side_effects=True),
        name="exchange",
    )(band_blocks, retained)
    tile = 2 * block
    total = (rows + 2 * depth) * block
    middle = (rows + depth) * block
    inside = pl.BlockSpec(memory_space=pltpu.VMEM)
    return pl.pallas_call(
        functools.partial(purify, (rows, reach, block, piece)),
        out_shape=jax.ShapeDtypeStruct((rows, band, piece, block), dtype),
        in_specs=[pl.BlockSpec(memory_space=pltpu.SMEM), inside, inside],
        out_specs=inside,
        scratch_shapes=[
            pltpu.VMEM((total, total), dtype),
            pltpu.VMEM((middle, total), dtype),
            pltpu.VMEM((tile, (reach + 1) * tile), dtype),
            pltpu.VMEM((rows * piece, middle), dtype),
            pltpu.VMEM((rows * piece, middle), dtype),
        ],
        compiler_params=pltpu.CompilerParams(vmem_limit_bytes=60 * 1024 * 1024),
        name="purify",
    )(flags, band_blocks, halo)


def solution(mesh):
    return jax.shard_map(
        functools.partial(per_device, mesh.shape["layer"], mesh.shape["grid"]),
        mesh=mesh,
        in_specs=(P("grid", None, None, None), P("grid", None)),
        out_specs=P("grid", None, "layer", None),
        check_vma=False,
    )
```

```python
import functools

import jax
import jax.numpy as jnp
from jax import lax
from jax.experimental import pallas as pl
from jax.experimental.pallas import tpu as pltpu
from jax.sharding import PartitionSpec as P

MESH = pl.DeviceIdType.MESH


def purify(dims, x_hbm, r_hbm, o_ref, x_ref, halo, flags, r3, wide, cur, strip, part, part_square,
           send, recv, r_send, r_recv, local):
    layers, grids, rows, reach, block = dims
    piece = block // layers
    band = 2 * reach + 1
    depth = 2 * reach
    tile = 2 * block
    span = reach // 2
    scale = 1.0 / (4.0 * band * block)
    total = rows + 2 * depth
    tiles = rows // 2
    mids = tiles + 2 * span
    centre = mids // 2

    q = lax.axis_index("layer")
    g = lax.axis_index("grid")
    right = lax.rem(g + 1, grids)
    left = lax.rem(g + grids - 1, grids)
    far = lax.rem(q + layers // 2, layers)
    near = q + 1 - 2 * lax.rem(q, 2)

    own_flags = pltpu.make_async_copy(r_hbm, r3.at[1], local.at[0])
    own_flags.start()
    own_blocks = pltpu.make_async_copy(x_hbm, x_ref, local.at[1])
    own_blocks.start()

    barrier = pltpu.get_barrier_semaphore()
    peers = ((q, left), (q, right), (far, g), (near, g))
    for peer in peers:
        pl.semaphore_signal(barrier, inc=1, device_id=peer, device_id_type=MESH)
    pl.semaphore_wait(barrier, len(peers))

    mine = pl.ds(pl.multiple_of(q * piece, piece), piece)
    fars = pl.ds(pl.multiple_of(far * piece, piece), piece)

    def copy(stage, side, j, source, target, peer):
        return pltpu.make_async_remote_copy(
            src_ref=source,
            dst_ref=target,
            send_sem=send.at[stage, side, j],
            recv_sem=recv.at[stage, side, j],
            device_id=peer,
            device_id_type=MESH,
        )

    sides = ((q, right), (q, left))
    copies = {}
    flag_copies = []
    for side in range(2):
        flag_copies.append(
            pltpu.make_async_remote_copy(
                src_ref=r_hbm,
                dst_ref=flags.at[side],
                send_sem=r_send.at[side],
                recv_sem=r_recv.at[side],
                device_id=sides[side],
                device_id_type=MESH,
            )
        )
    for j in range(depth):
        count = min(reach + 1, j + 1)
        for side in range(2):
            there = halo.at[side, j, 0:count, mine, :]
            beyond = halo.at[side, j, 0:count, fars, :]
            if side == 0:
                source = x_hbm.at[rows - 1 - j, reach : reach + count, mine, :]
            else:
                source = x_hbm.at[j, reach + 1 - count : reach + 1, mine, :]
            copies[0, side, j] = copy(0, side, j, source, there, sides[side])
            copies[1, side, j] = copy(1, side, j, there, there, (far, g))
            copies[2, side, j] = copy(2, side, j, there, there, (near, g))
            copies[3, side, j] = copy(3, side, j, beyond, beyond, (near, g))
            copies[0, side, j].start()
        if j == 1:
            for side in range(2):
                flag_copies[side].start()

    def forward(*js):
        for j in js:
            for side in range(2):
                copies[0, side, j].wait_recv()
                copies[1, side, j].start()
                copies[2, side, j].start()

    def share(*js):
        for j in js:
            for side in range(2):
                copies[1, side, j].wait_recv()
                copies[3, side, j].start()

    def masked(value, r, w):
        place = r + rows
        return jnp.where(r3[place // rows, place % rows, w] != 0, value, jnp.zeros_like(value))

    def put(r, c, value):
        wide[
            (r + depth) * block : (r + depth + 1) * block,
            (c + depth) * block : (c + depth + 1) * block,
        ] = value

    def build(*js):
        for j in js:
            for side in range(2):
                copies[2, side, j].wait_recv()
                copies[3, side, j].wait_recv()
                count = min(reach + 1, j + 1)
                r = -1 - j if side == 0 else rows + j
                for s in range(count):
                    w = reach + s if side == 0 else reach + 1 - count + s
                    c = r + w - reach
                    value = masked(halo[side, j, s], r, w)
                    put(r, c, value)
                    if c != r:
                        put(c, r, value.T)

    def ranges(d):
        low = max(0, d - span)
        high = min(2 * span, d + span)
        return low, high + 1

    def step(i):
        rows_at = slice((i + span) * tile, (i + span + 1) * tile)
        for d in range(2 * span + 1):
            low, high = ranges(d)
            inner = slice((i + low) * tile, (i + high) * tile)
            columns = slice((i + d) * tile, (i + d + 1) * tile)
            product = jnp.dot(
                wide[rows_at, inner], wide[inner, columns], preferred_element_type=jnp.float32
            )
            for a in range(2):
                for b in range(2):
                    w = 2 * (d - span) + b - a + reach
                    if 0 <= w < band:
                        value = masked(
                            product[a * block : (a + 1) * block, b * block : (b + 1) * block],
                            2 * i - reach + a,
                            w,
                        ).astype(jnp.bfloat16)
                    else:
                        value = jnp.zeros((block, block), jnp.bfloat16)
                    at = d * tile + b * block
                    strip[a * block : (a + 1) * block, at : at + block] = value
        for d in range(2 * span + 1):
            if not 0 <= i + d - span < mids:
                continue
            low, high = ranges(d)
            inner = slice((i + low) * tile, (i + high) * tile)
            columns = slice((i + d) * tile, (i + d + 1) * tile)
            product = jnp.dot(
                strip[:, low * tile : high * tile],
                wide[inner, columns],
                preferred_element_type=jnp.float32,
            )
            value = (3.0 * wide[rows_at, columns].astype(jnp.float32) - product * scale) * 0.5
            for a in range(2):
                for b in range(2):
                    w = 2 * (d - span) + b - a + reach
                    if 0 <= w < band:
                        result = masked(
                            value[a * block : (a + 1) * block, b * block : (b + 1) * block],
                            2 * i - reach + a,
                            w,
                        ).astype(jnp.bfloat16)
                    else:
                        result = jnp.zeros((block, block), jnp.bfloat16)
                    down = i * tile + a * block
                    at = (i + d - span) * tile + b * block
                    cur[down : down + block, at : at + block] = result

    empty = jnp.zeros((block, block), jnp.bfloat16)
    for t in range(total // 2):
        r = 2 * t - depth
        if r + reach + 1 < rows + depth:
            put(r, r + reach + 1, empty)
        if r - reach >= -depth:
            put(r + 1, r - reach, empty)
    own_flags.wait()
    own_blocks.wait()
    for r in range(rows):
        for w in range(band):
            c = r + w - reach
            value = masked(x_ref[r, w], r, w)
            put(r, c, value)
            if c < 0 or c >= rows:
                put(c, r, value.T)

    forward(*range(reach))
    step(centre)
    for side in range(2):
        flag_copies[side].wait_recv()
        landed = pltpu.make_async_copy(flags.at[side], r3.at[2 * side], local.at[0])
        landed.start()
        landed.wait()
    forward(reach)
    share(0, 1)
    forward(reach + 1)
    sent = 2
    for near_by in range(1, span + tiles // 2 + 1):
        build(*range(2 * near_by - 2, 2 * near_by))
        step(centre - near_by)
        ahead = reach + 1 + near_by
        if ahead < depth:
            forward(ahead)
        if sent < depth:
            share(sent, sent + 1)
            sent += 2
        step(centre + near_by)

    for r in range(rows):
        start = pl.multiple_of((r + reach) * block + q * piece, piece)
        for c in range(0, mids * 2):
            if 0 <= c - r < band:
                part[r * piece : (r + 1) * piece, c * block : (c + 1) * block] = cur[
                    pl.ds(start, piece), c * block : (c + 1) * block
                ]
            else:
                blank = jnp.zeros((piece, block), jnp.bfloat16)
                part[r * piece : (r + 1) * piece, c * block : (c + 1) * block] = blank
                part_square[r * piece : (r + 1) * piece, c * block : (c + 1) * block] = blank

    def columns_of(c, source):
        low, high = max(0, c - span), min(mids, c + span + 1)
        first, last = max(0, c - 2 * span), min(tiles, c + 1)
        product = jnp.dot(
            source[first * 2 * piece : last * 2 * piece, low * tile : high * tile],
            cur[low * tile : high * tile, c * tile : (c + 1) * tile],
            preferred_element_type=jnp.float32,
        )
        for r in range(2 * first, 2 * last):
            for b in range(2):
                w = 2 * c + b - r
                if 0 <= w < band:
                    at = (r - 2 * first) * piece
                    yield r, w, product[at : at + piece, b * block : (b + 1) * block]

    for c in range(mids):
        for r, w, value in columns_of(c, part):
            part_square[
                r * piece : (r + 1) * piece, (r + w) * block : (r + w + 1) * block
            ] = masked(value, r, w).astype(jnp.bfloat16)
    for c in range(mids):
        for r, w, value in columns_of(c, part_square):
            before = part[r * piece : (r + 1) * piece, (r + w) * block : (r + w + 1) * block]
            after = (3.0 * before.astype(jnp.float32) - value * scale) * 0.5
            o_ref[r, w] = masked(after, r, w).astype(jnp.bfloat16)

    for j in range(depth):
        for side in range(2):
            for stage in range(4):
                copies[stage, side, j].wait_send()
    for side in range(2):
        flag_copies[side].wait_send()


def per_device(layers, grids, band_blocks, retained):
    rows, band, block, _ = band_blocks.shape
    reach = (band - 1) // 2
    depth = 2 * reach
    piece = block // layers
    dtype = band_blocks.dtype
    anywhere = pl.BlockSpec(memory_space=pl.ANY)
    tile = 2 * block
    total = (rows + 2 * depth) * block
    middle = (rows + depth) * block
    return pl.pallas_call(
        functools.partial(purify, (layers, grids, rows, reach, block)),
        out_shape=jax.ShapeDtypeStruct((rows, band, piece, block), dtype),
        in_specs=[anywhere, anywhere],
        out_specs=pl.BlockSpec(memory_space=pltpu.VMEM),
        scratch_shapes=[
            pltpu.VMEM((rows, band, block, block), dtype),
            pltpu.VMEM((2, depth, reach + 1, block, block), dtype),
            pltpu.VMEM((2, rows, band), retained.dtype),
            pltpu.SMEM((3, rows, band), retained.dtype),
            pltpu.VMEM((total, total), dtype),
            pltpu.VMEM((middle, middle), dtype),
            pltpu.VMEM((tile, (reach + 1) * tile), dtype),
            pltpu.VMEM((rows * piece, middle), dtype),
            pltpu.VMEM((rows * piece, middle), dtype),
            pltpu.SemaphoreType.DMA((4, 2, depth)),
            pltpu.SemaphoreType.DMA((4, 2, depth)),
            pltpu.SemaphoreType.DMA((2,)),
            pltpu.SemaphoreType.DMA((2,)),
            pltpu.SemaphoreType.DMA((2,)),
        ],
        compiler_params=pltpu.CompilerParams(
            collective_id=0, has_side_effects=True, vmem_limit_bytes=60 * 1024 * 1024
        ),
        name="purify",
    )(band_blocks, retained)


def solution(mesh):
    return jax.shard_map(
        functools.partial(per_device, mesh.shape["layer"], mesh.shape["grid"]),
        mesh=mesh,
        in_specs=(P("grid", None, None, None), P("grid", None)),
        out_specs=P("grid", None, "layer", None),
        check_vma=False,
    )
```

```python
import functools

import jax
import jax.numpy as jnp
from jax import lax
from jax.experimental import pallas as pl
from jax.experimental.pallas import tpu as pltpu
from jax.sharding import PartitionSpec as P

MESH = pl.DeviceIdType.MESH


def purify(dims, x_hbm, r_hbm, o_ref, x_ref, halo, flags, r3, wide, cur, strip, part, part_square,
           send, recv, r_send, r_recv, local):
    layers, grids, rows, reach, block = dims
    piece = block // layers
    band = 2 * reach + 1
    depth = 2 * reach
    tile = 2 * block
    span = reach // 2
    scale = 1.0 / (4.0 * band * block)
    total = rows + 2 * depth
    tiles = rows // 2
    mids = tiles + 2 * span
    centre = mids // 2

    q = lax.axis_index("layer")
    g = lax.axis_index("grid")
    right = lax.rem(g + 1, grids)
    left = lax.rem(g + grids - 1, grids)
    far = lax.rem(q + layers // 2, layers)
    near = q + 1 - 2 * lax.rem(q, 2)

    own_flags = pltpu.make_async_copy(r_hbm, r3.at[1], local.at[0])
    own_flags.start()
    own_blocks = pltpu.make_async_copy(x_hbm, x_ref, local.at[1])
    own_blocks.start()

    barrier = pltpu.get_barrier_semaphore()
    peers = ((q, left), (q, right), (far, g), (near, g))
    for peer in peers:
        pl.semaphore_signal(barrier, inc=1, device_id=peer, device_id_type=MESH)
    pl.semaphore_wait(barrier, len(peers))

    mine = pl.ds(pl.multiple_of(q * piece, piece), piece)
    fars = pl.ds(pl.multiple_of(far * piece, piece), piece)

    def copy(stage, side, j, source, target, peer):
        return pltpu.make_async_remote_copy(
            src_ref=source,
            dst_ref=target,
            send_sem=send.at[stage, side, j],
            recv_sem=recv.at[stage, side, j],
            device_id=peer,
            device_id_type=MESH,
        )

    sides = ((q, right), (q, left))
    copies = {}
    flag_copies = []
    for side in range(2):
        flag_copies.append(
            pltpu.make_async_remote_copy(
                src_ref=r_hbm,
                dst_ref=flags.at[side],
                send_sem=r_send.at[side],
                recv_sem=r_recv.at[side],
                device_id=sides[side],
                device_id_type=MESH,
            )
        )
    for j in range(depth):
        count = min(reach + 1, j + 1)
        for side in range(2):
            there = halo.at[side, j, 0:count, mine, :]
            beyond = halo.at[side, j, 0:count, fars, :]
            if side == 0:
                source = x_hbm.at[rows - 1 - j, reach : reach + count]
            else:
                source = x_hbm.at[j, reach + 1 - count : reach + 1]
            copies[0, side, j] = copy(0, side, j, source.at[:, mine, :], there, sides[side])
            if j < depth - 1:
                copies[1, side, j] = copy(1, side, j, there, there, (far, g))
            else:
                copies[1, side, j] = copy(
                    1, side, j, source.at[:, fars, :], beyond, sides[side]
                )
            copies[2, side, j] = copy(2, side, j, there, there, (near, g))
            copies[3, side, j] = copy(3, side, j, beyond, beyond, (near, g))
            copies[0, side, j].start()
            if j == depth - 1:
                copies[1, side, j].start()
        if j == 1:
            for side in range(2):
                flag_copies[side].start()

    def forward(*js):
        for j in js:
            for side in range(2):
                copies[0, side, j].wait_recv()
                if j < depth - 1:
                    copies[1, side, j].start()
                copies[2, side, j].start()

    def share(*js):
        for j in js:
            for side in range(2):
                copies[1, side, j].wait_recv()
                copies[3, side, j].start()

    def masked(value, r, w):
        place = r + rows
        return jnp.where(r3[place // rows, place % rows, w] != 0, value, jnp.zeros_like(value))

    def put(r, c, value):
        wide[
            (r + depth) * block : (r + depth + 1) * block,
            (c + depth) * block : (c + depth + 1) * block,
        ] = value

    def build(*js):
        for j in js:
            for side in range(2):
                copies[2, side, j].wait_recv()
                copies[3, side, j].wait_recv()
                count = min(reach + 1, j + 1)
                r = -1 - j if side == 0 else rows + j
                for s in range(count):
                    w = reach + s if side == 0 else reach + 1 - count + s
                    c = r + w - reach
                    value = masked(halo[side, j, s], r, w)
                    put(r, c, value)
                    if c != r:
                        put(c, r, value.T)

    def ranges(d):
        low = max(0, d - span)
        high = min(2 * span, d + span)
        return low, high + 1

    every = range(2 * span + 1)

    def squares(i, which):
        rows_at = slice((i + span) * tile, (i + span + 1) * tile)
        for d in which:
            low, high = ranges(d)
            inner = slice((i + low) * tile, (i + high) * tile)
            columns = slice((i + d) * tile, (i + d + 1) * tile)
            product = jnp.dot(
                wide[rows_at, inner], wide[inner, columns], preferred_element_type=jnp.float32
            )
            for a in range(2):
                for b in range(2):
                    w = 2 * (d - span) + b - a + reach
                    if 0 <= w < band:
                        value = masked(
                            product[a * block : (a + 1) * block, b * block : (b + 1) * block],
                            2 * i - reach + a,
                            w,
                        ).astype(jnp.bfloat16)
                    else:
                        value = jnp.zeros((block, block), jnp.bfloat16)
                    at = d * tile + b * block
                    strip[i, a * block : (a + 1) * block, at : at + block] = value

    def cubes(i):
        rows_at = slice((i + span) * tile, (i + span + 1) * tile)
        for d in every:
            if not 0 <= i + d - span < mids:
                continue
            low, high = ranges(d)
            inner = slice((i + low) * tile, (i + high) * tile)
            columns = slice((i + d) * tile, (i + d + 1) * tile)
            product = jnp.dot(
                strip[i, :, low * tile : high * tile],
                wide[inner, columns],
                preferred_element_type=jnp.float32,
            )
            value = (3.0 * wide[rows_at, columns].astype(jnp.float32) - product * scale) * 0.5
            for a in range(2):
                for b in range(2):
                    w = 2 * (d - span) + b - a + reach
                    if 0 <= w < band:
                        result = masked(
                            value[a * block : (a + 1) * block, b * block : (b + 1) * block],
                            2 * i - reach + a,
                            w,
                        ).astype(jnp.bfloat16)
                    else:
                        result = jnp.zeros((block, block), jnp.bfloat16)
                    down = i * tile + a * block
                    at = (i + d - span) * tile + b * block
                    cur[down : down + block, at : at + block] = result

    def early(i):
        if span <= i < span + tiles:
            return [d for d in every if span <= i + d - span < span + tiles]
        return [d for d in every if (d > span if i < centre else d < span)]

    def rest(i):
        squares(i, [d for d in every if d not in early(i)])
        cubes(i)

    empty = jnp.zeros((block, block), jnp.bfloat16)
    for t in range(total // 2):
        r = 2 * t - depth
        if r + reach + 1 < rows + depth:
            put(r, r + reach + 1, empty)
        if r - reach >= -depth:
            put(r + 1, r - reach, empty)
    own_flags.wait()
    own_blocks.wait()
    for r in range(rows):
        for w in range(band):
            c = r + w - reach
            value = masked(x_ref[r, w], r, w)
            put(r, c, value)
            if c < 0 or c >= rows:
                put(c, r, value.T)

    def gather():
        for r in range(rows):
            start = pl.multiple_of((r + reach) * block + q * piece, piece)
            for c in range(0, mids * 2):
                if 0 <= c - r < band:
                    part[r * piece : (r + 1) * piece, c * block : (c + 1) * block] = cur[
                        pl.ds(start, piece), c * block : (c + 1) * block
                    ]
                else:
                    blank = jnp.zeros((piece, block), jnp.bfloat16)
                    part[r * piece : (r + 1) * piece, c * block : (c + 1) * block] = blank
                    part_square[r * piece : (r + 1) * piece, c * block : (c + 1) * block] = blank

    def columns_of(c, source):
        low, high = max(0, c - span), min(mids, c + span + 1)
        first, last = max(0, c - 2 * span), min(tiles, c + 1)
        product = jnp.dot(
            source[first * 2 * piece : last * 2 * piece, low * tile : high * tile],
            cur[low * tile : high * tile, c * tile : (c + 1) * tile],
            preferred_element_type=jnp.float32,
        )
        for r in range(2 * first, 2 * last):
            for b in range(2):
                w = 2 * c + b - r
                if 0 <= w < band:
                    at = (r - 2 * first) * piece
                    yield r, w, product[at : at + piece, b * block : (b + 1) * block]

    def part_squares(which):
        for c in which:
            for r, w, value in columns_of(c, part):
                part_square[
                    r * piece : (r + 1) * piece, (r + w) * block : (r + w + 1) * block
                ] = masked(value, r, w).astype(jnp.bfloat16)

    squares(centre, every)
    cubes(centre)
    forward(0, 1)
    squares(centre - 1, early(centre - 1))
    forward(2)
    squares(centre + 1, early(centre + 1))
    squares(centre - 2, early(centre - 2))
    forward(3)
    share(0, 1)
    squares(centre + 2, early(centre + 2))
    for side in range(2):
        flag_copies[side].wait_recv()
        landed = pltpu.make_async_copy(flags.at[side], r3.at[2 * side], local.at[0])
        landed.start()
        landed.wait()
    build(0, 1)
    rest(centre - 1)
    forward(4)
    share(2)
    rest(centre + 1)
    share(3)
    forward(5)
    build(2, 3)
    rest(centre - 2)
    forward(6)
    share(4)
    rest(centre + 2)
    forward(7)
    share(5)
    squares(centre - 3, early(centre - 3))
    squares(centre + 3, early(centre + 3))
    gather()
    share(7)
    build(4, 5)
    rest(centre - 3)
    share(6)
    rest(centre + 3)
    squares(centre - 4, early(centre - 4))
    squares(centre + 4, early(centre + 4))
    inner_columns = range(centre - 1, centre + 2)
    part_squares(inner_columns)
    build(6, 7)
    rest(centre - 4)
    rest(centre + 4)
    part_squares([c for c in range(mids) if c not in inner_columns])

    for c in range(mids):
        for r, w, value in columns_of(c, part_square):
            before = part[r * piece : (r + 1) * piece, (r + w) * block : (r + w + 1) * block]
            after = (3.0 * before.astype(jnp.float32) - value * scale) * 0.5
            o_ref[r, w] = masked(after, r, w).astype(jnp.bfloat16)

    for j in range(depth):
        for side in range(2):
            for stage in range(4):
                copies[stage, side, j].wait_send()
    for side in range(2):
        flag_copies[side].wait_send()


def per_device(layers, grids, band_blocks, retained):
    rows, band, block, _ = band_blocks.shape
    reach = (band - 1) // 2
    depth = 2 * reach
    piece = block // layers
    dtype = band_blocks.dtype
    anywhere = pl.BlockSpec(memory_space=pl.ANY)
    tile = 2 * block
    total = (rows + 2 * depth) * block
    middle = (rows + depth) * block
    return pl.pallas_call(
        functools.partial(purify, (layers, grids, rows, reach, block)),
        out_shape=jax.ShapeDtypeStruct((rows, band, piece, block), dtype),
        in_specs=[anywhere, anywhere],
        out_specs=pl.BlockSpec(memory_space=pltpu.VMEM),
        scratch_shapes=[
            pltpu.VMEM((rows, band, block, block), dtype),
            pltpu.VMEM((2, depth, reach + 1, block, block), dtype),
            pltpu.VMEM((2, rows, band), retained.dtype),
            pltpu.SMEM((3, rows, band), retained.dtype),
            pltpu.VMEM((total, total), dtype),
            pltpu.VMEM((middle, middle), dtype),
            pltpu.VMEM((middle // tile, tile, (reach + 1) * tile), dtype),
            pltpu.VMEM((rows * piece, middle), dtype),
            pltpu.VMEM((rows * piece, middle), dtype),
            pltpu.SemaphoreType.DMA((4, 2, depth)),
            pltpu.SemaphoreType.DMA((4, 2, depth)),
            pltpu.SemaphoreType.DMA((2,)),
            pltpu.SemaphoreType.DMA((2,)),
            pltpu.SemaphoreType.DMA((2,)),
        ],
        compiler_params=pltpu.CompilerParams(
            collective_id=0, has_side_effects=True, vmem_limit_bytes=60 * 1024 * 1024
        ),
        name="purify",
    )(band_blocks, retained)


def solution(mesh):
    return jax.shard_map(
        functools.partial(per_device, mesh.shape["layer"], mesh.shape["grid"]),
        mesh=mesh,
        in_specs=(P("grid", None, None, None), P("grid", None)),
        out_specs=P("grid", None, "layer", None),
        check_vma=False,
    )
```

```python
import functools

import jax
import jax.numpy as jnp
from jax import lax
from jax.experimental import pallas as pl
from jax.experimental.pallas import tpu as pltpu
from jax.sharding import PartitionSpec as P

MESH = pl.DeviceIdType.MESH


def purify(dims, x_hbm, r_hbm, o_ref, x_ref, halo, flags, r3, wide, cur, strip, part, part_square,
           send, recv, r_send, r_recv, local):
    layers, grids, rows, reach, block = dims
    piece = block // layers
    band = 2 * reach + 1
    depth = 2 * reach
    tile = 2 * block
    span = reach // 2
    scale = 1.0 / (4.0 * band * block)
    total = rows + 2 * depth
    tiles = rows // 2
    mids = tiles + 2 * span
    centre = mids // 2

    q = lax.axis_index("layer")
    g = lax.axis_index("grid")
    right = lax.rem(g + 1, grids)
    left = lax.rem(g + grids - 1, grids)
    far = lax.rem(q + layers // 2, layers)
    near = q + 1 - 2 * lax.rem(q, 2)

    own_flags = pltpu.make_async_copy(r_hbm, r3.at[1], local.at[0])
    own_flags.start()
    own_blocks = pltpu.make_async_copy(x_hbm, x_ref, local.at[1])
    own_blocks.start()

    barrier = pltpu.get_barrier_semaphore()
    peers = ((q, left), (q, right), (far, g), (near, g))
    for peer in peers:
        pl.semaphore_signal(barrier, inc=1, device_id=peer, device_id_type=MESH)
    pl.semaphore_wait(barrier, len(peers))

    mine = pl.ds(pl.multiple_of(q * piece, piece), piece)
    fars = pl.ds(pl.multiple_of(far * piece, piece), piece)

    def copy(stage, side, j, source, target, peer):
        return pltpu.make_async_remote_copy(
            src_ref=source,
            dst_ref=target,
            send_sem=send.at[stage, side, j],
            recv_sem=recv.at[stage, side, j],
            device_id=peer,
            device_id_type=MESH,
        )

    sides = ((q, right), (q, left))
    copies = {}
    flag_copies = []
    for side in range(2):
        flag_copies.append(
            pltpu.make_async_remote_copy(
                src_ref=r_hbm,
                dst_ref=flags.at[side],
                send_sem=r_send.at[side],
                recv_sem=r_recv.at[side],
                device_id=sides[side],
                device_id_type=MESH,
            )
        )
    for j in range(depth):
        count = min(reach + 1, j + 1)
        for side in range(2):
            there = halo.at[side, j, 0:count, mine, :]
            beyond = halo.at[side, j, 0:count, fars, :]
            if side == 0:
                source = x_hbm.at[rows - 1 - j, reach : reach + count]
            else:
                source = x_hbm.at[j, reach + 1 - count : reach + 1]
            copies[0, side, j] = copy(0, side, j, source.at[:, mine, :], there, sides[side])
            copies[1, side, j] = copy(1, side, j, there, there, (far, g))
            copies[2, side, j] = copy(2, side, j, there, there, (near, g))
            copies[3, side, j] = copy(3, side, j, beyond, beyond, (near, g))
            copies[0, side, j].start()
        if j == 1:
            for side in range(2):
                flag_copies[side].start()

    def forward(*js):
        for j in js:
            for side in range(2):
                copies[0, side, j].wait_recv()
                copies[1, side, j].start()
                copies[2, side, j].start()

    def share(*js):
        for j in js:
            for side in range(2):
                copies[1, side, j].wait_recv()
                copies[3, side, j].start()

    def masked(value, r, w):
        place = r + rows
        return jnp.where(r3[place // rows, place % rows, w] != 0, value, jnp.zeros_like(value))

    def put(r, c, value):
        wide[
            (r + depth) * block : (r + depth + 1) * block,
            (c + depth) * block : (c + depth + 1) * block,
        ] = value

    def build(*js):
        for j in js:
            for side in range(2):
                copies[2, side, j].wait_recv()
                copies[3, side, j].wait_recv()
                count = min(reach + 1, j + 1)
                r = -1 - j if side == 0 else rows + j
                for s in range(count):
                    w = reach + s if side == 0 else reach + 1 - count + s
                    c = r + w - reach
                    value = masked(halo[side, j, s], r, w)
                    put(r, c, value)
                    if c != r:
                        put(c, r, value.T)

    def ranges(d):
        low = max(0, d - span)
        high = min(2 * span, d + span)
        return low, high + 1

    every = range(2 * span + 1)

    def squares(i, which):
        rows_at = slice((i + span) * tile, (i + span + 1) * tile)
        for d in which:
            low, high = ranges(d)
            inner = slice((i + low) * tile, (i + high) * tile)
            columns = slice((i + d) * tile, (i + d + 1) * tile)
            product = jnp.dot(
                wide[rows_at, inner], wide[inner, columns], preferred_element_type=jnp.float32
            )
            for a in range(2):
                for b in range(2):
                    w = 2 * (d - span) + b - a + reach
                    if 0 <= w < band:
                        value = masked(
                            product[a * block : (a + 1) * block, b * block : (b + 1) * block],
                            2 * i - reach + a,
                            w,
                        ).astype(jnp.bfloat16)
                    else:
                        value = jnp.zeros((block, block), jnp.bfloat16)
                    at = d * tile + b * block
                    strip[i, a * block : (a + 1) * block, at : at + block] = value

    def cubes(i):
        rows_at = slice((i + span) * tile, (i + span + 1) * tile)
        for d in every:
            if not 0 <= i + d - span < mids:
                continue
            low, high = ranges(d)
            inner = slice((i + low) * tile, (i + high) * tile)
            columns = slice((i + d) * tile, (i + d + 1) * tile)
            product = jnp.dot(
                strip[i, :, low * tile : high * tile],
                wide[inner, columns],
                preferred_element_type=jnp.float32,
            )
            value = (3.0 * wide[rows_at, columns].astype(jnp.float32) - product * scale) * 0.5
            for a in range(2):
                for b in range(2):
                    w = 2 * (d - span) + b - a + reach
                    if 0 <= w < band:
                        result = masked(
                            value[a * block : (a + 1) * block, b * block : (b + 1) * block],
                            2 * i - reach + a,
                            w,
                        ).astype(jnp.bfloat16)
                    else:
                        result = jnp.zeros((block, block), jnp.bfloat16)
                    down = i * tile + a * block
                    at = (i + d - span) * tile + b * block
                    cur[down : down + block, at : at + block] = result

    def early(i):
        if span <= i < span + tiles:
            return [d for d in every if span <= i + d - span < span + tiles]
        return [d for d in every if (d > span if i < centre else d < span)]

    def rest(i):
        squares(i, [d for d in every if d not in early(i)])
        cubes(i)

    empty = jnp.zeros((block, block), jnp.bfloat16)
    for t in range(total // 2):
        r = 2 * t - depth
        if r + reach + 1 < rows + depth:
            put(r, r + reach + 1, empty)
        if r - reach >= -depth:
            put(r + 1, r - reach, empty)
    own_flags.wait()
    own_blocks.wait()
    for r in range(rows):
        for w in range(band):
            c = r + w - reach
            value = masked(x_ref[r, w], r, w)
            put(r, c, value)
            if c < 0 or c >= rows:
                put(c, r, value.T)

    def gather():
        for r in range(rows):
            start = pl.multiple_of((r + reach) * block + q * piece, piece)
            for c in range(0, mids * 2):
                if 0 <= c - r < band:
                    part[r * piece : (r + 1) * piece, c * block : (c + 1) * block] = cur[
                        pl.ds(start, piece), c * block : (c + 1) * block
                    ]
                else:
                    blank = jnp.zeros((piece, block), jnp.bfloat16)
                    part[r * piece : (r + 1) * piece, c * block : (c + 1) * block] = blank
                    part_square[r * piece : (r + 1) * piece, c * block : (c + 1) * block] = blank

    def columns_of(c, source):
        low, high = max(0, c - span), min(mids, c + span + 1)
        first, last = max(0, c - 2 * span), min(tiles, c + 1)
        product = jnp.dot(
            source[first * 2 * piece : last * 2 * piece, low * tile : high * tile],
            cur[low * tile : high * tile, c * tile : (c + 1) * tile],
            preferred_element_type=jnp.float32,
        )
        for r in range(2 * first, 2 * last):
            for b in range(2):
                w = 2 * c + b - r
                if 0 <= w < band:
                    at = (r - 2 * first) * piece
                    yield r, w, product[at : at + piece, b * block : (b + 1) * block]

    def part_squares(which):
        for c in which:
            for r, w, value in columns_of(c, part):
                part_square[
                    r * piece : (r + 1) * piece, (r + w) * block : (r + w + 1) * block
                ] = masked(value, r, w).astype(jnp.bfloat16)

    squares(centre, every)
    cubes(centre)
    forward(0, 1)
    squares(centre - 1, early(centre - 1))
    forward(2)
    squares(centre + 1, early(centre + 1))
    squares(centre - 2, early(centre - 2))
    forward(3)
    share(0, 1)
    squares(centre + 2, early(centre + 2))
    for side in range(2):
        flag_copies[side].wait_recv()
        landed = pltpu.make_async_copy(flags.at[side], r3.at[2 * side], local.at[0])
        landed.start()
        landed.wait()
    build(0, 1)
    rest(centre - 1)
    forward(4)
    share(2)
    rest(centre + 1)
    share(3)
    forward(5)
    build(2, 3)
    rest(centre - 2)
    forward(6)
    share(4)
    rest(centre + 2)
    forward(7)
    share(5)
    squares(centre - 3, early(centre - 3))
    squares(centre + 3, early(centre + 3))
    gather()
    build(4, 5)
    rest(centre - 3)
    share(6)
    rest(centre + 3)
    share(7)
    squares(centre - 4, early(centre - 4))
    squares(centre + 4, early(centre + 4))
    inner_columns = range(centre - 1, centre + 2)
    part_squares(inner_columns)
    build(6, 7)
    rest(centre - 4)
    rest(centre + 4)
    part_squares([c for c in range(mids) if c not in inner_columns])

    for c in range(mids):
        for r, w, value in columns_of(c, part_square):
            before = part[r * piece : (r + 1) * piece, (r + w) * block : (r + w + 1) * block]
            after = (3.0 * before.astype(jnp.float32) - value * scale) * 0.5
            o_ref[r, w] = masked(after, r, w).astype(jnp.bfloat16)

    for j in range(depth):
        for side in range(2):
            for stage in range(4):
                copies[stage, side, j].wait_send()
    for side in range(2):
        flag_copies[side].wait_send()


def per_device(layers, grids, band_blocks, retained):
    rows, band, block, _ = band_blocks.shape
    reach = (band - 1) // 2
    depth = 2 * reach
    piece = block // layers
    dtype = band_blocks.dtype
    anywhere = pl.BlockSpec(memory_space=pl.ANY)
    tile = 2 * block
    total = (rows + 2 * depth) * block
    middle = (rows + depth) * block
    return pl.pallas_call(
        functools.partial(purify, (layers, grids, rows, reach, block)),
        out_shape=jax.ShapeDtypeStruct((rows, band, piece, block), dtype),
        in_specs=[anywhere, anywhere],
        out_specs=pl.BlockSpec(memory_space=pltpu.VMEM),
        scratch_shapes=[
            pltpu.VMEM((rows, band, block, block), dtype),
            pltpu.VMEM((2, depth, reach + 1, block, block), dtype),
            pltpu.VMEM((2, rows, band), retained.dtype),
            pltpu.SMEM((3, rows, band), retained.dtype),
            pltpu.VMEM((total, total), dtype),
            pltpu.VMEM((middle, middle), dtype),
            pltpu.VMEM((middle // tile, tile, (reach + 1) * tile), dtype),
            pltpu.VMEM((rows * piece, middle), dtype),
            pltpu.VMEM((rows * piece, middle), dtype),
            pltpu.SemaphoreType.DMA((4, 2, depth)),
            pltpu.SemaphoreType.DMA((4, 2, depth)),
            pltpu.SemaphoreType.DMA((2,)),
            pltpu.SemaphoreType.DMA((2,)),
            pltpu.SemaphoreType.DMA((2,)),
        ],
        compiler_params=pltpu.CompilerParams(
            collective_id=0, has_side_effects=True, vmem_limit_bytes=60 * 1024 * 1024
        ),
        name="purify",
    )(band_blocks, retained)


def solution(mesh):
    return jax.shard_map(
        functools.partial(per_device, mesh.shape["layer"], mesh.shape["grid"]),
        mesh=mesh,
        in_specs=(P("grid", None, None, None), P("grid", None)),
        out_specs=P("grid", None, "layer", None),
        check_vma=False,
    )
```
